32 devices in a mesh: groups: 2 (over y), ctx: 8 (over z, x), head: 2 (over core).
Axes of the slice: x: 2, y: 2, z: 4, core: 2. Of those that a mesh axis runs over, the one named last changes fastest.
Arguments:
- queries: bfloat16 [2048, 2048], P(('groups', 'ctx'), 'head'), parts along dimension 0, may hold values from -6 to 6
- key_rows: bfloat16 [2048, 2048], P(('groups', 'ctx'), 'head'), parts along dimension 0, may hold values from -6 to 6
- value_rows: bfloat16 [2048, 2048], P(('groups', 'ctx'), 'head'), parts along dimension 0, may hold values from -6 to 6
- out_grad: bfloat16 [2048, 2048], P(('groups', 'ctx'), 'head'), parts along dimension 0, may hold values from -6 to 6
Outputs:
- attended: bfloat16 [2048, 2048], P(('groups', 'ctx'), 'head'), parts along dimension 0
- query_grad: bfloat16 [2048, 2048], P(('groups', 'ctx'), 'head'), parts along dimension 0
- key_grad: bfloat16 [2048, 2048], P(('groups', 'ctx'), 'head'), parts along dimension 0
- value_grad: bfloat16 [2048, 2048], P(('groups', 'ctx'), 'head'), parts along dimension 0
The draws below stay inside these ranges and needn't reach their ends.
There are 2 independent parts, one for each index of `groups`. The reference program is written for one: setup_inputs(seed, part) draws one part's arguments, and reference() takes and returns one part's arrays. A program takes and returns all parts, laid end to end along the dimension named above; each array names one. Nothing has to cross between parts.
All inputs are finite; a program needn't handle non-finite values.
Results may differ from the reference program's by a relative error of at most 0.033.
Values may be sent and summed in bfloat16 or wider, within the bound.
A program may use at most 128 MiB of HBM per device.

```python
import jax
import jax.numpy as jnp
from jax import lax

HEADS = 16
HEAD_DIM = 128
BLK = 128
TOKENS = 1024


def base_rows(key, spread):
    width = HEADS * HEAD_DIM
    values = jax.random.normal(key, (TOKENS, width), jnp.float32)
    return jnp.clip(values * spread, -6.0, 6.0)


def draw_queries(key, part):
    rows = base_rows(jax.random.fold_in(key, 1), 2.0)
    return rows.astype(jnp.bfloat16)


def draw_key_rows(key, part):
    rows = base_rows(jax.random.fold_in(key, 2), 1.0)
    return rows.astype(jnp.bfloat16)


def levels(key, dims, cuts, low, top_value):
    def one(axis_at, blocks):
        steps = jax.random.uniform(jax.random.fold_in(jax.random.fold_in(key, 6), axis_at), (blocks,), jnp.float32, low / len(cuts), top_value / len(cuts))
        return jnp.repeat(jnp.exp(steps), dims[axis_at] // blocks).reshape((-1,) + (1,) * (len(dims) - axis_at - 1))

    level = one(*cuts[0])
    for cut in cuts[1:]:
        level = level * one(*cut)
    return level


def centred(stream_key, dims, scale, limit, pieces=(), kind=jnp.bfloat16):
    values = jax.random.normal(stream_key, dims, jnp.float32) * scale
    if len(pieces) > 0:
        values = levels(stream_key, dims, pieces, -0.22, 0.18) * values
    return jnp.clip(values, min=-limit, max=limit).astype(kind)


def setup_inputs(seed: int = 0, part: int = 0) -> dict:
    key_list = jax.random.split(jax.random.key(seed), 5)
    part_keys = jax.random.split(jax.random.fold_in(key_list[4], part), 5)
    return {
        "queries": draw_queries(jax.random.fold_in(jax.random.fold_in(key_list[4], part), 71), part),
        "key_rows": draw_key_rows(jax.random.fold_in(jax.random.fold_in(key_list[4], part), 71), part),
        "value_rows": centred(part_keys[2], (TOKENS, HEADS * HEAD_DIM), 1.0, 6.0, ((0, 8), (1, 2))),
        "out_grad": centred(part_keys[3], (TOKENS, HEADS * HEAD_DIM), 1.0, 6.0, ((0, 8), (1, 2))),
    }


def offset_list(count):
    result = [0]
    width = 1
    while width < count // 2:
        result = result + [width, -width]
        width = width * 2
    result.append(count // 2)
    return result


def rounded(values):
    return lax.optimization_barrier(values.astype(jnp.bfloat16)).astype(jnp.float32)


def reference(queries, key_rows, value_rows, out_grad):
    blocks = TOKENS // BLK
    shaped = (blocks, BLK, HEADS, HEAD_DIM)
    query_all = queries.reshape(shaped).astype(jnp.float32)
    key_all = key_rows.reshape(shaped).astype(jnp.float32)
    value_all = value_rows.reshape(shaped).astype(jnp.float32)
    grad_all = out_grad.reshape(shaped).astype(jnp.float32)
    scaling = HEAD_DIM ** -0.5
    shifts = offset_list(blocks)

    def scores_at(offset):
        moved = jnp.roll(key_all, -offset, axis=0)
        return jnp.einsum("bqhd,bkhd->bhqk", query_all, moved) * scaling

    peak = jnp.full((blocks, HEADS, BLK), -jnp.inf, jnp.float32)
    total = jnp.zeros((blocks, HEADS, BLK), jnp.float32)
    for offset in shifts:
        scores = scores_at(offset)
        new_peak = jnp.maximum(peak, scores.max(-1))
        total = total * jnp.exp(peak - new_peak) + jnp.exp(scores - new_peak[..., None]).sum(-1)
        peak = new_peak
    row_lse = peak + jnp.log(total)

    summed = jnp.zeros(shaped, jnp.float32)
    for offset in shifts:
        weights = rounded(jnp.exp(scores_at(offset) - row_lse[..., None]))
        summed = summed + jnp.einsum("bhqk,bkhd->bqhd", weights, jnp.roll(value_all, -offset, axis=0))
    attended = summed.astype(jnp.bfloat16)
    delta = jnp.einsum("bqhd,bqhd->bhq", grad_all, attended.astype(jnp.float32))

    query_sum = jnp.zeros(shaped, jnp.float32)
    key_sum = jnp.zeros(shaped, jnp.float32)
    value_sum = jnp.zeros(shaped, jnp.float32)
    for offset in shifts:
        key_moved = jnp.roll(key_all, -offset, axis=0)
        value_moved = jnp.roll(value_all, -offset, axis=0)
        probs = jnp.exp(scores_at(offset) - row_lse[..., None])
        weights = rounded(probs)
        dprob = jnp.einsum("bqhd,bkhd->bhqk", grad_all, value_moved)
        dscore = rounded(probs * (dprob - delta[..., None]))
        query_sum = query_sum + jnp.einsum("bhqk,bkhd->bqhd", dscore, key_moved)
        key_term = rounded(jnp.einsum("bhqk,bqhd->bkhd", dscore, query_all) * scaling)
        value_term = rounded(jnp.einsum("bhqk,bqhd->bkhd", weights, grad_all))
        key_sum = key_sum + jnp.roll(key_term, offset, axis=0)
        value_sum = value_sum + jnp.roll(value_term, offset, axis=0)
    flat = (TOKENS, HEADS * HEAD_DIM)
    return (attended.reshape(flat),
            (query_sum * scaling).astype(jnp.bfloat16).reshape(flat),
            key_sum.astype(jnp.bfloat16).reshape(flat),
            value_sum.astype(jnp.bfloat16).reshape(flat))
```

```python
import functools
import math

import jax
import jax.numpy as jnp
from jax import lax
from jax.experimental import pallas as pl
from jax.experimental.pallas import tpu as pltpu
from jax.sharding import PartitionSpec as P

HEAD_DIM = 128


def shifted(block, axis, distance):
    devices = range(lax.axis_size(axis))
    route = [((i - distance) % len(devices), i) for i in devices]
    return lax.ppermute(block, axis, route)


def offset_list(count):
    result = [0]
    width = 1
    while width < count // 2:
        result = result + [width, -width]
        width = width * 2
    result.append(count // 2)
    return result


def block_scores(query_part, key_part, scaling):
    return (
        jnp.einsum("qhd,khd->hqk", query_part, key_part, preferred_element_type=jnp.float32)
        * scaling
    )


def permuted(queries, key_rows, value_rows, out_grad):
    rows = queries.shape[0]
    width_all = queries.shape[1]
    heads_here = width_all // HEAD_DIM
    shaped = (rows, heads_here, HEAD_DIM)
    query_here = queries.reshape(shaped)
    grad_here = out_grad.reshape(shaped)
    count = lax.axis_size("ctx")
    shifts = offset_list(count)
    scaling = HEAD_DIM ** (-0.5)
    blocks_seen = len(shifts)
    fetched = [shifted((key_rows, value_rows), "ctx", -offset) for offset in shifts[1:]]
    key_stack = jnp.stack([key_rows] + [pair[0] for pair in fetched]).reshape(
        (blocks_seen,) + shaped
    )
    value_stack = jnp.stack([value_rows] + [pair[1] for pair in fetched]).reshape(
        (blocks_seen,) + shaped
    )

    def pass_one(carry, key_block):
        peak, total = carry
        scores = block_scores(query_here, key_block, scaling)
        new_peak = jnp.maximum(peak, scores.max(-1))
        total = total * jnp.exp(peak - new_peak) + jnp.exp(scores - new_peak[..., None]).sum(-1)
        return ((new_peak, total), None)

    start_peak = jnp.full((heads_here, rows), -jnp.inf, jnp.float32)
    start_total = jnp.zeros((heads_here, rows), jnp.float32)
    (peak, total), unused = lax.scan(pass_one, (start_peak, start_total), key_stack)
    row_lse = peak + jnp.log(total)

    def pass_two(summed, blocks):
        key_block, value_block = blocks
        weights = jnp.exp(block_scores(query_here, key_block, scaling) - row_lse[..., None]).astype(
            jnp.bfloat16
        )
        summed = summed + jnp.einsum(
            "hqk,khd->qhd", weights, value_block, preferred_element_type=jnp.float32
        )
        return (summed, None)

    summed, unused = lax.scan(pass_two, jnp.zeros(shaped, jnp.float32), (key_stack, value_stack))
    attended = summed.astype(jnp.bfloat16)
    delta = jnp.einsum("qhd,qhd->hq", grad_here.astype(jnp.float32), attended.astype(jnp.float32))

    def query_side(key_block, value_block):
        probs = jnp.exp(block_scores(query_here, key_block, scaling) - row_lse[..., None])
        weights = probs.astype(jnp.bfloat16)
        dprob = jnp.einsum(
            "qhd,khd->hqk", grad_here, value_block, preferred_element_type=jnp.float32
        )
        dscore = (probs * (dprob - delta[..., None])).astype(jnp.bfloat16)
        return (weights, dscore)

    def pass_three(query_sum, blocks):
        key_block, value_block = blocks
        weights, dscore = query_side(key_block, value_block)
        query_sum = query_sum + jnp.einsum(
            "hqk,khd->qhd", dscore, key_block, preferred_element_type=jnp.float32
        )
        key_term = (
            jnp.einsum("hqk,qhd->khd", dscore, query_here, preferred_element_type=jnp.float32)
            * scaling
        ).astype(jnp.bfloat16)
        value_term = jnp.einsum(
            "hqk,qhd->khd", weights, grad_here, preferred_element_type=jnp.float32
        ).astype(jnp.bfloat16)
        return (query_sum, (key_term, value_term))

    query_sum, terms = lax.scan(
        pass_three, jnp.zeros(shaped, jnp.float32), (key_stack, value_stack)
    )
    key_terms, value_terms = terms
    key_sum = lax.optimization_barrier(key_terms[0]).astype(jnp.float32)
    value_sum = lax.optimization_barrier(value_terms[0]).astype(jnp.float32)
    for index in range(1, blocks_seen):
        moved = shifted((key_terms[index], value_terms[index]), "ctx", shifts[index])
        key_sum = key_sum + moved[0].astype(jnp.float32)
        value_sum = value_sum + moved[1].astype(jnp.float32)
    flat = (rows, width_all)
    return (
        attended.reshape(flat),
        (query_sum * scaling).astype(jnp.bfloat16).reshape(flat),
        key_sum.astype(jnp.bfloat16).reshape(flat),
        value_sum.astype(jnp.bfloat16).reshape(flat),
    )


def dot(a, b, dims):
    return lax.dot_general(a, b, (dims, ((), ())), preferred_element_type=jnp.float32)


def exchange_kernel(
    n,
    shifts,
    q_in,
    k_in,
    v_in,
    g_in,
    o_out,
    dq_out,
    dk_out,
    dv_out,
    qb,
    kb,
    vb,
    gb,
    qt,
    gt,
    wb,
    sb,
    ob,
    dqb,
    dkb,
    dvb,
    in_send,
    in_recv,
    out_send,
    out_recv,
    ends_sem,
):
    me = lax.axis_index("ctx")
    scaling = HEAD_DIM ** (-0.5)

    def partner(d):
        total, bit = 0, 1
        while bit < n:
            total = total + bit * ((me // bit + d // bit) % 2)
            bit *= 2
        return total

    quarter = n // 4
    same = [s for s in range(1, n) if s // quarter in (0, 3)]
    cross = [s for s in range(1, n) if s // quarter in (1, 2)]
    zone = me // quarter
    middle = jnp.logical_or(zone == 1, zone == 2)

    def tell(sem, s):
        pl.semaphore_signal(
            sem, inc=1, device_id={"ctx": partner(s)}, device_id_type=pl.DeviceIdType.MESH
        )

    barrier = pltpu.get_barrier_semaphore()
    for s in same:
        tell(barrier, s)

    def columns(index):
        return pl.ds(pl.multiple_of(index * HEAD_DIM, HEAD_DIM), HEAD_DIM)

    inward = ((k_in, kb), (q_in, qb), (v_in, vb), (g_in, gb))
    outward = ((ob, o_out), (dvb, dv_out), (dqb, dq_out), (dkb, dk_out))

    def in_copy(t, s):
        source, place = inward[t]
        peer = partner(s)
        return pltpu.make_async_remote_copy(
            src_ref=source.at[:, columns(peer)],
            dst_ref=place.at[me],
            send_sem=in_send.at[t],
            recv_sem=in_recv.at[t],
            device_id={"ctx": peer},
            device_id_type=pl.DeviceIdType.MESH,
        )

    def in_own(t):
        source, place = inward[t]
        return pltpu.make_async_copy(source.at[:, columns(me)], place.at[me], in_recv.at[t])

    def out_copy(t, s):
        source, place = outward[t]
        peer = partner(s)
        return pltpu.make_async_remote_copy(
            src_ref=source.at[peer],
            dst_ref=place.at[:, columns(me)],
            send_sem=out_send.at[t],
            recv_sem=out_recv.at[t],
            device_id={"ctx": peer},
            device_id_type=pl.DeviceIdType.MESH,
        )

    def out_own(t):
        source, place = outward[t]
        return pltpu.make_async_copy(source.at[me], place.at[:, columns(me)], out_recv.at[t])

    @pl.when(middle)
    def _():
        pl.semaphore_wait(barrier, len(same))
        tell(barrier, quarter)
        for t in range(4):
            for s in reversed(same):
                in_copy(t, s).start()
        pl.semaphore_wait(ends_sem, 1)
        for t in range(4):
            for s in reversed(cross):
                in_copy(t, s).start()

    @pl.when(jnp.logical_not(middle))
    def _():
        pl.semaphore_wait(barrier, len(same) + 1)
        tell(ends_sem, quarter)
        for t in range(4):
            for s in reversed(range(1, n)):
                in_copy(t, s).start()

    for t in range(4):
        in_own(t).start()

    def arrive(t):
        whole = inward[t][1]
        pltpu.make_async_copy(whole, whole, in_recv.at[t]).wait()

    def each_block(body):
        lax.fori_loop(0, n, lambda step, c: (body(step), c)[1], 0)

    def flips(step):
        return partner(step)

    def send(t, step):
        s = flips(step)

        @pl.when(s > 0)
        def _():
            out_copy(t, s).start()

        @pl.when(s == 0)
        def _():
            out_own(t).start()

    def near(index, sign=1):
        return [lax.rem(index + sign * d + n, n) for d in shifts]

    def rows_of(buf, index):
        return jnp.concatenate([buf[j] for j in near(index)], axis=0)

    arrive(0)
    arrive(1)

    def scores(i):
        q = qb[i]
        s = dot(q, rows_of(kb, i), ((1,), (1,)))
        peak = jnp.max(s, axis=-1, keepdims=True)
        e = jnp.exp2((s - peak) * (scaling * math.log2(math.e)))
        w = (e * (1.0 / jnp.sum(e, axis=-1, keepdims=True))).astype(jnp.bfloat16)
        for m in range(len(shifts)):
            wb[i, m] = w[:, m * 128 : (m + 1) * 128]
        qt[i] = q.T

    each_block(scores)
    arrive(2)

    def block_weights(ref, i):
        return jnp.concatenate([ref[i, m] for m in range(len(shifts))], axis=1)

    def attend(step):
        i = partner(flips(step))
        o = dot(block_weights(wb, i), rows_of(vb, i), ((1,), (0,)))
        ob[i] = o.astype(jnp.bfloat16)
        send(0, step)

    each_block(attend)
    arrive(3)

    def transpose_grad(i):
        gt[i] = gb[i].T

    each_block(transpose_grad)

    def value_side(step):
        j = partner(flips(step))
        from_blocks = near(j, -1)
        left = jnp.concatenate([gt[i] for i in from_blocks], axis=1)
        right = jnp.concatenate([wb[i, m] for m, i in enumerate(from_blocks)], axis=0)
        dvb[j] = dot(left, right, ((1,), (0,))).T.astype(jnp.bfloat16)
        send(1, step)

    each_block(value_side)

    def query_side(step):
        i = partner(flips(step))
        g = gb[i]
        delta = jnp.sum(g.astype(jnp.float32) * ob[i].astype(jnp.float32), axis=-1, keepdims=True)
        dprob = dot(g, rows_of(vb, i), ((1,), (1,)))
        ds = (block_weights(wb, i).astype(jnp.float32) * (dprob - delta)).astype(jnp.bfloat16)
        for m in range(len(shifts)):
            sb[i, m] = ds[:, m * 128 : (m + 1) * 128]
        dqb[i] = (dot(ds, rows_of(kb, i), ((1,), (0,))) * scaling).astype(jnp.bfloat16)
        send(2, step)

    each_block(query_side)

    def key_side(step):
        j = partner(flips(step))
        from_blocks = near(j, -1)
        left = jnp.concatenate([qt[i] for i in from_blocks], axis=1)
        right = jnp.concatenate([sb[i, m] for m, i in enumerate(from_blocks)], axis=0)
        dkb[j] = (dot(left, right, ((1,), (0,))) * scaling).T.astype(jnp.bfloat16)
        send(3, step)

    each_block(key_side)

    for t in range(4):
        sent = inward[t][1].at[pl.ds(0, n - 1)]
        pltpu.make_async_copy(sent, sent, in_send.at[t]).wait()
    for t in range(4):
        sent = outward[t][0].at[pl.ds(0, n - 1)]
        pltpu.make_async_copy(sent, sent, out_send.at[t]).wait()
        whole = outward[t][1]
        pltpu.make_async_copy(whole, whole, out_recv.at[t]).wait()


def exchanged(queries, key_rows, value_rows, out_grad):
    rows = queries.shape[0]
    n = lax.axis_size("ctx")
    shifts = offset_list(n)
    seen = len(shifts)
    block = (n, rows, HEAD_DIM)
    bf16 = jnp.bfloat16
    return pl.pallas_call(
        functools.partial(exchange_kernel, n, shifts),
        out_shape=tuple(jax.ShapeDtypeStruct(queries.shape, bf16) for _ in range(4)),
        in_specs=[pl.BlockSpec(memory_space=pltpu.HBM)] * 4,
        out_specs=tuple(pl.BlockSpec(memory_space=pl.ANY) for _ in range(4)),
        scratch_shapes=[pltpu.VMEM(block, bf16)] * 4
        + [pltpu.VMEM((n, HEAD_DIM, rows), bf16)] * 2
        + [pltpu.VMEM((n, seen, rows, rows), bf16)] * 2
        + [pltpu.VMEM(block, bf16)] * 4
        + [pltpu.SemaphoreType.DMA((4,))] * 4
        + [pltpu.SemaphoreType.REGULAR],
        compiler_params=pltpu.CompilerParams(
            collective_id=0, has_side_effects=True, vmem_limit_bytes=40 * 2**20
        ),
    )(*[pltpu.with_memory_space_constraint(x, pltpu.HBM) for x in (queries, key_rows, value_rows, out_grad)])


def store_kernel(*refs):
    sems = refs[8]
    copies = [pltpu.make_async_copy(refs[t], refs[4 + t], sems.at[t]) for t in range(4)]
    for c in copies:
        c.start()
    for c in copies:
        c.wait()


def stored(arrays):
    return pl.pallas_call(
        store_kernel,
        out_shape=tuple(jax.ShapeDtypeStruct(a.shape, a.dtype) for a in arrays),
        in_specs=[pl.BlockSpec(memory_space=pl.ANY)] * 4,
        out_specs=tuple(pl.BlockSpec(memory_space=pl.ANY) for _ in range(4)),
        scratch_shapes=[pltpu.SemaphoreType.DMA((4,))],
    )(*[pltpu.with_memory_space_constraint(a, pltpu.VMEM) for a in arrays])


def per_device(queries, key_rows, value_rows, out_grad):
    rows, width = queries.shape
    count = lax.axis_size("ctx")
    if rows == HEAD_DIM and count * HEAD_DIM == width and count >= 4 and count & (count - 1) == 0:
        return tuple(stored(exchanged(queries, key_rows, value_rows, out_grad)))
    return permuted(queries, key_rows, value_rows, out_grad)


def solution(mesh):
    return jax.shard_map(
        per_device,
        mesh=mesh,
        in_specs=(
            P(("groups", "ctx"), "head"),
            P(("groups", "ctx"), "head"),
            P(("groups", "ctx"), "head"),
            P(("groups", "ctx"), "head"),
        ),
        out_specs=(
            P(("groups", "ctx"), "head"),
            P(("groups", "ctx"), "head"),
            P(("groups", "ctx"), "head"),
            P(("groups", "ctx"), "head"),
        ),
        check_vma=False,
    )
```

```python
import functools
import math

import jax
import jax.numpy as jnp
from jax import lax
from jax.experimental import pallas as pl
from jax.experimental.pallas import tpu as pltpu
from jax.sharding import PartitionSpec as P

HEAD_DIM = 128


def shifted(block, axis, distance):
    devices = range(lax.axis_size(axis))
    route = [((i - distance) % len(devices), i) for i in devices]
    return lax.ppermute(block, axis, route)


def offset_list(count):
    result = [0]
    width = 1
    while width < count // 2:
        result = result + [width, -width]
        width = width * 2
    result.append(count // 2)
    return result


def block_scores(query_part, key_part, scaling):
    return (
        jnp.einsum("qhd,khd->hqk", query_part, key_part, preferred_element_type=jnp.float32)
        * scaling
    )


def permuted(queries, key_rows, value_rows, out_grad):
    rows = queries.shape[0]
    width_all = queries.shape[1]
    heads_here = width_all // HEAD_DIM
    shaped = (rows, heads_here, HEAD_DIM)
    query_here = queries.reshape(shaped)
    grad_here = out_grad.reshape(shaped)
    count = lax.axis_size("ctx")
    shifts = offset_list(count)
    scaling = HEAD_DIM ** (-0.5)
    blocks_seen = len(shifts)
    fetched = [shifted((key_rows, value_rows), "ctx", -offset) for offset in shifts[1:]]
    key_stack = jnp.stack([key_rows] + [pair[0] for pair in fetched]).reshape(
        (blocks_seen,) + shaped
    )
    value_stack = jnp.stack([value_rows] + [pair[1] for pair in fetched]).reshape(
        (blocks_seen,) + shaped
    )

    def pass_one(carry, key_block):
        peak, total = carry
        scores = block_scores(query_here, key_block, scaling)
        new_peak = jnp.maximum(peak, scores.max(-1))
        total = total * jnp.exp(peak - new_peak) + jnp.exp(scores - new_peak[..., None]).sum(-1)
        return ((new_peak, total), None)

    start_peak = jnp.full((heads_here, rows), -jnp.inf, jnp.float32)
    start_total = jnp.zeros((heads_here, rows), jnp.float32)
    (peak, total), unused = lax.scan(pass_one, (start_peak, start_total), key_stack)
    row_lse = peak + jnp.log(total)

    def pass_two(summed, blocks):
        key_block, value_block = blocks
        weights = jnp.exp(block_scores(query_here, key_block, scaling) - row_lse[..., None]).astype(
            jnp.bfloat16
        )
        summed = summed + jnp.einsum(
            "hqk,khd->qhd", weights, value_block, preferred_element_type=jnp.float32
        )
        return (summed, None)

    summed, unused = lax.scan(pass_two, jnp.zeros(shaped, jnp.float32), (key_stack, value_stack))
    attended = summed.astype(jnp.bfloat16)
    delta = jnp.einsum("qhd,qhd->hq", grad_here.astype(jnp.float32), attended.astype(jnp.float32))

    def query_side(key_block, value_block):
        probs = jnp.exp(block_scores(query_here, key_block, scaling) - row_lse[..., None])
        weights = probs.astype(jnp.bfloat16)
        dprob = jnp.einsum(
            "qhd,khd->hqk", grad_here, value_block, preferred_element_type=jnp.float32
        )
        dscore = (probs * (dprob - delta[..., None])).astype(jnp.bfloat16)
        return (weights, dscore)

    def pass_three(query_sum, blocks):
        key_block, value_block = blocks
        weights, dscore = query_side(key_block, value_block)
        query_sum = query_sum + jnp.einsum(
            "hqk,khd->qhd", dscore, key_block, preferred_element_type=jnp.float32
        )
        key_term = (
            jnp.einsum("hqk,qhd->khd", dscore, query_here, preferred_element_type=jnp.float32)
            * scaling
        ).astype(jnp.bfloat16)
        value_term = jnp.einsum(
            "hqk,qhd->khd", weights, grad_here, preferred_element_type=jnp.float32
        ).astype(jnp.bfloat16)
        return (query_sum, (key_term, value_term))

    query_sum, terms = lax.scan(
        pass_three, jnp.zeros(shaped, jnp.float32), (key_stack, value_stack)
    )
    key_terms, value_terms = terms
    key_sum = lax.optimization_barrier(key_terms[0]).astype(jnp.float32)
    value_sum = lax.optimization_barrier(value_terms[0]).astype(jnp.float32)
    for index in range(1, blocks_seen):
        moved = shifted((key_terms[index], value_terms[index]), "ctx", shifts[index])
        key_sum = key_sum + moved[0].astype(jnp.float32)
        value_sum = value_sum + moved[1].astype(jnp.float32)
    flat = (rows, width_all)
    return (
        attended.reshape(flat),
        (query_sum * scaling).astype(jnp.bfloat16).reshape(flat),
        key_sum.astype(jnp.bfloat16).reshape(flat),
        value_sum.astype(jnp.bfloat16).reshape(flat),
    )


def dot(a, b, dims):
    return lax.dot_general(a, b, (dims, ((), ())), preferred_element_type=jnp.float32)


def exchange_kernel(
    n,
    shifts,
    q_in,
    k_in,
    v_in,
    g_in,
    o_out,
    dq_out,
    dk_out,
    dv_out,
    qb,
    kb,
    vb,
    gb,
    qt,
    gt,
    wb,
    sb,
    ob,
    dqb,
    dkb,
    dvb,
    in_send,
    in_recv,
    out_send,
    out_recv,
    ends_sem,
):
    me = lax.axis_index("ctx")
    scaling = HEAD_DIM ** (-0.5)

    def partner(d):
        total, bit = 0, 1
        while bit < n:
            total = total + bit * ((me // bit + d // bit) % 2)
            bit *= 2
        return total

    quarter = n // 4
    same = [s for s in range(1, n) if s // quarter in (0, 3)]
    cross = [s for s in range(1, n) if s // quarter in (1, 2)]
    zone = me // quarter
    middle = jnp.logical_or(zone == 1, zone == 2)

    def tell(sem, s):
        pl.semaphore_signal(
            sem, inc=1, device_id={"ctx": partner(s)}, device_id_type=pl.DeviceIdType.MESH
        )

    barrier = pltpu.get_barrier_semaphore()
    for s in same:
        tell(barrier, s)

    def columns(index):
        return pl.ds(pl.multiple_of(index * HEAD_DIM, HEAD_DIM), HEAD_DIM)

    inward = ((k_in, kb), (q_in, qb), (v_in, vb), (g_in, gb))
    outward = ((ob, o_out), (dvb, dv_out), (dqb, dq_out), (dkb, dk_out))

    def in_copy(t, s):
        source, place = inward[t]
        peer = partner(s)
        return pltpu.make_async_remote_copy(
            src_ref=source.at[:, columns(peer)],
            dst_ref=place.at[me],
            send_sem=in_send.at[t],
            recv_sem=in_recv.at[t],
            device_id={"ctx": peer},
            device_id_type=pl.DeviceIdType.MESH,
        )

    def in_own(t):
        source, place = inward[t]
        return pltpu.make_async_copy(source.at[:, columns(me)], place.at[me], in_recv.at[t])

    def out_copy(t, s):
        source, place = outward[t]
        peer = partner(s)
        return pltpu.make_async_remote_copy(
            src_ref=source.at[peer],
            dst_ref=place.at[:, columns(me)],
            send_sem=out_send.at[t],
            recv_sem=out_recv.at[t],
            device_id={"ctx": peer},
            device_id_type=pl.DeviceIdType.MESH,
        )

    def out_own(t):
        source, place = outward[t]
        return pltpu.make_async_copy(source.at[me], place.at[:, columns(me)], out_recv.at[t])

    @pl.when(middle)
    def _():
        pl.semaphore_wait(barrier, len(same))
        tell(barrier, quarter)
        for t in range(4):
            for s in reversed(same):
                in_copy(t, s).start()
        pl.semaphore_wait(ends_sem, 1)
        for t in range(4):
            for s in reversed(cross):
                in_copy(t, s).start()

    @pl.when(jnp.logical_not(middle))
    def _():
        pl.semaphore_wait(barrier, len(same) + 1)
        tell(ends_sem, quarter)
        for t in range(4):
            for s in reversed(range(1, n)):
                in_copy(t, s).start()

    for t in range(4):
        in_own(t).start()

    def arrive(t):
        whole = inward[t][1]
        pltpu.make_async_copy(whole, whole, in_recv.at[t]).wait()

    def each_block(body):
        lax.fori_loop(0, n, lambda step, c: (body(step), c)[1], 0)

    def flips(step):
        return partner(step)

    def send(t, step):
        s = flips(step)

        @pl.when(s > 0)
        def _():
            out_copy(t, s).start()

        @pl.when(s == 0)
        def _():
            out_own(t).start()

    def near(index, sign=1):
        return [lax.rem(index + sign * d + n, n) for d in shifts]

    def rows_of(buf, index):
        return jnp.concatenate([buf[j] for j in near(index)], axis=0)

    arrive(0)
    arrive(1)

    def scores(i):
        q = qb[i]
        s = dot(q, rows_of(kb, i), ((1,), (1,)))
        peak = jnp.max(s, axis=-1, keepdims=True)
        e = jnp.exp2((s - peak) * (scaling * math.log2(math.e)))
        w = (e * (1.0 / jnp.sum(e, axis=-1, keepdims=True))).astype(jnp.bfloat16)
        for m in range(len(shifts)):
            wb[i, m] = w[:, m * 128 : (m + 1) * 128]
        qt[i] = q.T

    each_block(scores)
    arrive(2)

    def block_weights(ref, i):
        return jnp.concatenate([ref[i, m] for m in range(len(shifts))], axis=1)

    def attend(step):
        i = partner(flips(step))
        o = dot(block_weights(wb, i), rows_of(vb, i), ((1,), (0,)))
        ob[i] = o.astype(jnp.bfloat16)
        send(0, step)

    each_block(attend)
    arrive(3)

    def transpose_grad(i):
        gt[i] = gb[i].T

    each_block(transpose_grad)

    def value_side(step):
        j = partner(flips(step))
        from_blocks = near(j, -1)
        left = jnp.concatenate([gt[i] for i in from_blocks], axis=1)
        right = jnp.concatenate([wb[i, m] for m, i in enumerate(from_blocks)], axis=0)
        dvb[j] = dot(left, right, ((1,), (0,))).T.astype(jnp.bfloat16)
        send(1, step)

    each_block(value_side)

    def query_side(step):
        i = partner(flips(step))
        g = gb[i]
        delta = jnp.sum(g.astype(jnp.float32) * ob[i].astype(jnp.float32), axis=-1, keepdims=True)
        dprob = dot(g, rows_of(vb, i), ((1,), (1,)))
        ds = (block_weights(wb, i).astype(jnp.float32) * (dprob - delta)).astype(jnp.bfloat16)
        for m in range(len(shifts)):
            sb[i, m] = ds[:, m * 128 : (m + 1) * 128]
        dqb[i] = (dot(ds, rows_of(kb, i), ((1,), (0,))) * scaling).astype(jnp.bfloat16)

    each_block(query_side)

    def key_side(step):
        j = partner(flips(step))
        from_blocks = near(j, -1)
        left = jnp.concatenate([qt[i] for i in from_blocks], axis=1)
        right = jnp.concatenate([sb[i, m] for m, i in enumerate(from_blocks)], axis=0)
        dkb[j] = (dot(left, right, ((1,), (0,))) * scaling).T.astype(jnp.bfloat16)
        send(2, step)
        send(3, step)

    each_block(key_side)

    for t in range(4):
        sent = inward[t][1].at[pl.ds(0, n - 1)]
        pltpu.make_async_copy(sent, sent, in_send.at[t]).wait()
    for t in range(4):
        sent = outward[t][0].at[pl.ds(0, n - 1)]
        pltpu.make_async_copy(sent, sent, out_send.at[t]).wait()
        whole = outward[t][1]
        pltpu.make_async_copy(whole, whole, out_recv.at[t]).wait()


def exchanged(queries, key_rows, value_rows, out_grad):
    rows = queries.shape[0]
    n = lax.axis_size("ctx")
    shifts = offset_list(n)
    seen = len(shifts)
    block = (n, rows, HEAD_DIM)
    bf16 = jnp.bfloat16
    return pl.pallas_call(
        functools.partial(exchange_kernel, n, shifts),
        out_shape=tuple(jax.ShapeDtypeStruct(queries.shape, bf16) for _ in range(4)),
        in_specs=[pl.BlockSpec(memory_space=pltpu.HBM)] * 4,
        out_specs=tuple(pl.BlockSpec(memory_space=pl.ANY) for _ in range(4)),
        scratch_shapes=[pltpu.VMEM(block, bf16)] * 4
        + [pltpu.VMEM((n, HEAD_DIM, rows), bf16)] * 2
        + [pltpu.VMEM((n, seen, rows, rows), bf16)] * 2
        + [pltpu.VMEM(block, bf16)] * 4
        + [pltpu.SemaphoreType.DMA((4,))] * 4
        + [pltpu.SemaphoreType.REGULAR],
        compiler_params=pltpu.CompilerParams(
            collective_id=0, has_side_effects=True, vmem_limit_bytes=40 * 2**20
        ),
    )(*[pltpu.with_memory_space_constraint(x, pltpu.HBM) for x in (queries, key_rows, value_rows, out_grad)])


def store_kernel(*refs):
    sems = refs[8]
    copies = [pltpu.make_async_copy(refs[t], refs[4 + t], sems.at[t]) for t in range(4)]
    for c in copies:
        c.start()
    for c in copies:
        c.wait()


def stored(arrays):
    return pl.pallas_call(
        store_kernel,
        out_shape=tuple(jax.ShapeDtypeStruct(a.shape, a.dtype) for a in arrays),
        in_specs=[pl.BlockSpec(memory_space=pl.ANY)] * 4,
        out_specs=tuple(pl.BlockSpec(memory_space=pl.ANY) for _ in range(4)),
        scratch_shapes=[pltpu.SemaphoreType.DMA((4,))],
    )(*[pltpu.with_memory_space_constraint(a, pltpu.VMEM) for a in arrays])


def per_device(queries, key_rows, value_rows, out_grad):
    rows, width = queries.shape
    count = lax.axis_size("ctx")
    if rows == HEAD_DIM and count * HEAD_DIM == width and count >= 4 and count & (count - 1) == 0:
        return tuple(stored(exchanged(queries, key_rows, value_rows, out_grad)))
    return permuted(queries, key_rows, value_rows, out_grad)


def solution(mesh):
    return jax.shard_map(
        per_device,
        mesh=mesh,
        in_specs=(
            P(("groups", "ctx"), "head"),
            P(("groups", "ctx"), "head"),
            P(("groups", "ctx"), "head"),
            P(("groups", "ctx"), "head"),
        ),
        out_specs=(
            P(("groups", "ctx"), "head"),
            P(("groups", "ctx"), "head"),
            P(("groups", "ctx"), "head"),
            P(("groups", "ctx"), "head"),
        ),
        check_vma=False,
    )
```

```python
import functools
import math

import jax
import jax.numpy as jnp
from jax import lax
from jax.experimental import pallas as pl
from jax.experimental.pallas import tpu as pltpu
from jax.sharding import PartitionSpec as P

HEAD_DIM = 128


def shifted(block, axis, distance):
    devices = range(lax.axis_size(axis))
    route = [((i - distance) % len(devices), i) for i in devices]
    return lax.ppermute(block, axis, route)


def offset_list(count):
    result = [0]
    width = 1
    while width < count // 2:
        result = result + [width, -width]
        width = width * 2
    result.append(count // 2)
    return result


def block_scores(query_part, key_part, scaling):
    return (
        jnp.einsum("qhd,khd->hqk", query_part, key_part, preferred_element_type=jnp.float32)
        * scaling
    )


def permuted(queries, key_rows, value_rows, out_grad):
    rows = queries.shape[0]
    width_all = queries.shape[1]
    heads_here = width_all // HEAD_DIM
    shaped = (rows, heads_here, HEAD_DIM)
    query_here = queries.reshape(shaped)
    grad_here = out_grad.reshape(shaped)
    count = lax.axis_size("ctx")
    shifts = offset_list(count)
    scaling = HEAD_DIM ** (-0.5)
    blocks_seen = len(shifts)
    fetched = [shifted((key_rows, value_rows), "ctx", -offset) for offset in shifts[1:]]
    key_stack = jnp.stack([key_rows] + [pair[0] for pair in fetched]).reshape(
        (blocks_seen,) + shaped
    )
    value_stack = jnp.stack([value_rows] + [pair[1] for pair in fetched]).reshape(
        (blocks_seen,) + shaped
    )

    def pass_one(carry, key_block):
        peak, total = carry
        scores = block_scores(query_here, key_block, scaling)
        new_peak = jnp.maximum(peak, scores.max(-1))
        total = total * jnp.exp(peak - new_peak) + jnp.exp(scores - new_peak[..., None]).sum(-1)
        return ((new_peak, total), None)

    start_peak = jnp.full((heads_here, rows), -jnp.inf, jnp.float32)
    start_total = jnp.zeros((heads_here, rows), jnp.float32)
    (peak, total), unused = lax.scan(pass_one, (start_peak, start_total), key_stack)
    row_lse = peak + jnp.log(total)

    def pass_two(summed, blocks):
        key_block, value_block = blocks
        weights = jnp.exp(block_scores(query_here, key_block, scaling) - row_lse[..., None]).astype(
            jnp.bfloat16
        )
        summed = summed + jnp.einsum(
            "hqk,khd->qhd", weights, value_block, preferred_element_type=jnp.float32
        )
        return (summed, None)

    summed, unused = lax.scan(pass_two, jnp.zeros(shaped, jnp.float32), (key_stack, value_stack))
    attended = summed.astype(jnp.bfloat16)
    delta = jnp.einsum("qhd,qhd->hq", grad_here.astype(jnp.float32), attended.astype(jnp.float32))

    def query_side(key_block, value_block):
        probs = jnp.exp(block_scores(query_here, key_block, scaling) - row_lse[..., None])
        weights = probs.astype(jnp.bfloat16)
        dprob = jnp.einsum(
            "qhd,khd->hqk", grad_here, value_block, preferred_element_type=jnp.float32
        )
        dscore = (probs * (dprob - delta[..., None])).astype(jnp.bfloat16)
        return (weights, dscore)

    def pass_three(query_sum, blocks):
        key_block, value_block = blocks
        weights, dscore = query_side(key_block, value_block)
        query_sum = query_sum + jnp.einsum(
            "hqk,khd->qhd", dscore, key_block, preferred_element_type=jnp.float32
        )
        key_term = (
            jnp.einsum("hqk,qhd->khd", dscore, query_here, preferred_element_type=jnp.float32)
            * scaling
        ).astype(jnp.bfloat16)
        value_term = jnp.einsum(
            "hqk,qhd->khd", weights, grad_here, preferred_element_type=jnp.float32
        ).astype(jnp.bfloat16)
        return (query_sum, (key_term, value_term))

    query_sum, terms = lax.scan(
        pass_three, jnp.zeros(shaped, jnp.float32), (key_stack, value_stack)
    )
    key_terms, value_terms = terms
    key_sum = lax.optimization_barrier(key_terms[0]).astype(jnp.float32)
    value_sum = lax.optimization_barrier(value_terms[0]).astype(jnp.float32)
    for index in range(1, blocks_seen):
        moved = shifted((key_terms[index], value_terms[index]), "ctx", shifts[index])
        key_sum = key_sum + moved[0].astype(jnp.float32)
        value_sum = value_sum + moved[1].astype(jnp.float32)
    flat = (rows, width_all)
    return (
        attended.reshape(flat),
        (query_sum * scaling).astype(jnp.bfloat16).reshape(flat),
        key_sum.astype(jnp.bfloat16).reshape(flat),
        value_sum.astype(jnp.bfloat16).reshape(flat),
    )


def dot(a, b, dims):
    return lax.dot_general(a, b, (dims, ((), ())), preferred_element_type=jnp.float32)


def exchange_kernel(
    n,
    shifts,
    q_in,
    k_in,
    v_in,
    g_in,
    o_out,
    dq_out,
    dk_out,
    dv_out,
    qb,
    kb,
    vb,
    gb,
    qt,
    gt,
    wb,
    sb,
    ob,
    dqb,
    dkb,
    dvb,
    in_send,
    in_recv,
    out_send,
    out_recv,
    ends_sem,
):
    me = lax.axis_index("ctx")
    scaling = HEAD_DIM ** (-0.5)

    def partner(d):
        total, bit = 0, 1
        while bit < n:
            total = total + bit * ((me // bit + d // bit) % 2)
            bit *= 2
        return total

    quarter = n // 4
    same = [s for s in range(1, n) if s // quarter in (0, 3)]
    opposite = 3 * quarter
    beside = range(quarter, 2 * quarter)
    zone = me // quarter
    middle = jnp.logical_or(zone == 1, zone == 2)

    def tell(sem, s):
        pl.semaphore_signal(
            sem, inc=1, device_id={"ctx": partner(s)}, device_id_type=pl.DeviceIdType.MESH
        )

    barrier = pltpu.get_barrier_semaphore()

    @pl.when(middle)
    def _():
        tell(barrier, opposite)

    @pl.when(jnp.logical_not(middle))
    def _():
        for s in same:
            tell(barrier, s)

    def columns(index):
        return pl.ds(pl.multiple_of(index * HEAD_DIM, HEAD_DIM), HEAD_DIM)

    inward = ((k_in, kb), (q_in, qb), (v_in, vb), (g_in, gb))
    outward = ((ob, o_out), (dvb, dv_out), (dqb, dq_out), (dkb, dk_out))

    def in_copy(t, s):
        source, place = inward[t]
        peer = partner(s)
        return pltpu.make_async_remote_copy(
            src_ref=source.at[:, columns(peer)],
            dst_ref=place.at[me],
            send_sem=in_send.at[t],
            recv_sem=in_recv.at[t],
            device_id={"ctx": peer},
            device_id_type=pl.DeviceIdType.MESH,
        )

    def in_own(t):
        source, place = inward[t]
        return pltpu.make_async_copy(source.at[:, columns(me)], place.at[me], in_recv.at[t])

    def out_copy(t, s):
        source, place = outward[t]
        peer = partner(s)
        return pltpu.make_async_remote_copy(
            src_ref=source.at[peer],
            dst_ref=place.at[:, columns(me)],
            send_sem=out_send.at[t],
            recv_sem=out_recv.at[t],
            device_id={"ctx": peer},
            device_id_type=pl.DeviceIdType.MESH,
        )

    def out_own(t):
        source, place = outward[t]
        return pltpu.make_async_copy(source.at[me], place.at[:, columns(me)], out_recv.at[t])

    def start(peers):
        for t in range(4):
            for s in peers:
                in_copy(t, s).start()

    @pl.when(middle)
    def _():
        pl.semaphore_wait(barrier, 1)
        start([opposite])
        for s in beside:
            tell(barrier, s)
        pl.semaphore_wait(ends_sem, 1)
        start([s for s in reversed(same) if s != opposite])
        start([s for s in range(n - 1, 0, -1) if s not in same])

    @pl.when(jnp.logical_not(middle))
    def _():
        pl.semaphore_wait(barrier, len(same) + quarter)
        tell(ends_sem, quarter)
        start(range(n - 1, 0, -1))

    for t in range(4):
        in_own(t).start()

    def arrive(t):
        whole = inward[t][1]
        pltpu.make_async_copy(whole, whole, in_recv.at[t]).wait()

    def each_block(body):
        lax.fori_loop(0, n, lambda step, c: (body(step), c)[1], 0)

    def flips(step):
        return partner(step)

    def send(t, step):
        s = flips(step)

        @pl.when(s > 0)
        def _():
            out_copy(t, s).start()

        @pl.when(s == 0)
        def _():
            out_own(t).start()

    def near(index, sign=1):
        return [lax.rem(index + sign * d + n, n) for d in shifts]

    def rows_of(buf, index):
        return jnp.concatenate([buf[j] for j in near(index)], axis=0)

    arrive(0)
    arrive(1)

    def scores(i):
        q = qb[i]
        s = dot(q, rows_of(kb, i), ((1,), (1,)))
        peak = jnp.max(s, axis=-1, keepdims=True)
        e = jnp.exp2((s - peak) * (scaling * math.log2(math.e)))
        w = (e * (1.0 / jnp.sum(e, axis=-1, keepdims=True))).astype(jnp.bfloat16)
        for m in range(len(shifts)):
            wb[i, m] = w[:, m * 128 : (m + 1) * 128]
        qt[i] = q.T

    each_block(scores)
    arrive(2)

    def block_weights(ref, i):
        return jnp.concatenate([ref[i, m] for m in range(len(shifts))], axis=1)

    def attend(step):
        i = partner(flips(step))
        o = dot(block_weights(wb, i), rows_of(vb, i), ((1,), (0,)))
        ob[i] = o.astype(jnp.bfloat16)
        send(0, step)

    each_block(attend)
    arrive(3)

    def transpose_grad(i):
        gt[i] = gb[i].T

    each_block(transpose_grad)

    def value_side(step):
        j = partner(flips(step))
        from_blocks = near(j, -1)
        left = jnp.concatenate([gt[i] for i in from_blocks], axis=1)
        right = jnp.concatenate([wb[i, m] for m, i in enumerate(from_blocks)], axis=0)
        dvb[j] = dot(left, right, ((1,), (0,))).T.astype(jnp.bfloat16)
        send(1, step)

    each_block(value_side)

    def query_side(step):
        i = partner(flips(step))
        g = gb[i]
        delta = jnp.sum(g.astype(jnp.float32) * ob[i].astype(jnp.float32), axis=-1, keepdims=True)
        dprob = dot(g, rows_of(vb, i), ((1,), (1,)))
        ds = (block_weights(wb, i).astype(jnp.float32) * (dprob - delta)).astype(jnp.bfloat16)
        for m in range(len(shifts)):
            sb[i, m] = ds[:, m * 128 : (m + 1) * 128]
        dqb[i] = (dot(ds, rows_of(kb, i), ((1,), (0,))) * scaling).astype(jnp.bfloat16)

    each_block(query_side)

    def key_side(step):
        j = partner(flips(step))
        from_blocks = near(j, -1)
        left = jnp.concatenate([qt[i] for i in from_blocks], axis=1)
        right = jnp.concatenate([sb[i, m] for m, i in enumerate(from_blocks)], axis=0)
        dkb[j] = (dot(left, right, ((1,), (0,))) * scaling).T.astype(jnp.bfloat16)
        send(2, step)
        send(3, step)

    each_block(key_side)

    for t in range(4):
        sent = inward[t][1].at[pl.ds(0, n - 1)]
        pltpu.make_async_copy(sent, sent, in_send.at[t]).wait()
    for t in range(4):
        sent = outward[t][0].at[pl.ds(0, n - 1)]
        pltpu.make_async_copy(sent, sent, out_send.at[t]).wait()
        whole = outward[t][1]
        pltpu.make_async_copy(whole, whole, out_recv.at[t]).wait()


def exchanged(queries, key_rows, value_rows, out_grad):
    rows = queries.shape[0]
    n = lax.axis_size("ctx")
    shifts = offset_list(n)
    seen = len(shifts)
    block = (n, rows, HEAD_DIM)
    bf16 = jnp.bfloat16
    return pl.pallas_call(
        functools.partial(exchange_kernel, n, shifts),
        out_shape=tuple(jax.ShapeDtypeStruct(queries.shape, bf16) for _ in range(4)),
        in_specs=[pl.BlockSpec(memory_space=pltpu.HBM)] * 4,
        out_specs=tuple(pl.BlockSpec(memory_space=pl.ANY) for _ in range(4)),
        scratch_shapes=[pltpu.VMEM(block, bf16)] * 4
        + [pltpu.VMEM((n, HEAD_DIM, rows), bf16)] * 2
        + [pltpu.VMEM((n, seen, rows, rows), bf16)] * 2
        + [pltpu.VMEM(block, bf16)] * 4
        + [pltpu.SemaphoreType.DMA((4,))] * 4
        + [pltpu.SemaphoreType.REGULAR],
        compiler_params=pltpu.CompilerParams(
            collective_id=0, has_side_effects=True, vmem_limit_bytes=40 * 2**20
        ),
    )(*[pltpu.with_memory_space_constraint(x, pltpu.HBM) for x in (queries, key_rows, value_rows, out_grad)])


def store_kernel(*refs):
    sems = refs[8]
    copies = [pltpu.make_async_copy(refs[t], refs[4 + t], sems.at[t]) for t in range(4)]
    for c in copies:
        c.start()
    for c in copies:
        c.wait()


def stored(arrays):
    return pl.pallas_call(
        store_kernel,
        out_shape=tuple(jax.ShapeDtypeStruct(a.shape, a.dtype) for a in arrays),
        in_specs=[pl.BlockSpec(memory_space=pl.ANY)] * 4,
        out_specs=tuple(pl.BlockSpec(memory_space=pl.ANY) for _ in range(4)),
        scratch_shapes=[pltpu.SemaphoreType.DMA((4,))],
    )(*[pltpu.with_memory_space_constraint(a, pltpu.VMEM) for a in arrays])


def per_device(queries, key_rows, value_rows, out_grad):
    rows, width = queries.shape
    count = lax.axis_size("ctx")
    if rows == HEAD_DIM and count * HEAD_DIM == width and count >= 4 and count & (count - 1) == 0:
        return tuple(stored(exchanged(queries, key_rows, value_rows, out_grad)))
    return permuted(queries, key_rows, value_rows, out_grad)


def solution(mesh):
    return jax.shard_map(
        per_device,
        mesh=mesh,
        in_specs=(
            P(("groups", "ctx"), "head"),
            P(("groups", "ctx"), "head"),
            P(("groups", "ctx"), "head"),
            P(("groups", "ctx"), "head"),
        ),
        out_specs=(
            P(("groups", "ctx"), "head"),
            P(("groups", "ctx"), "head"),
            P(("groups", "ctx"), "head"),
            P(("groups", "ctx"), "head"),
        ),
        check_vma=False,
    )
```

```python
import functools
import math

import jax
import jax.numpy as jnp
from jax import lax
from jax.experimental import pallas as pl
from jax.experimental.pallas import tpu as pltpu
from jax.sharding import PartitionSpec as P

HEAD_DIM = 128


def shifted(block, axis, distance):
    devices = range(lax.axis_size(axis))
    route = [((i - distance) % len(devices), i) for i in devices]
    return lax.ppermute(block, axis, route)


def offset_list(count):
    result = [0]
    width = 1
    while width < count // 2:
        result = result + [width, -width]
        width = width * 2
    result.append(count // 2)
    return result


def block_scores(query_part, key_part, scaling):
    return (
        jnp.einsum("qhd,khd->hqk", query_part, key_part, preferred_element_type=jnp.float32)
        * scaling
    )


def permuted(queries, key_rows, value_rows, out_grad):
    rows = queries.shape[0]
    width_all = queries.shape[1]
    heads_here = width_all // HEAD_DIM
    shaped = (rows, heads_here, HEAD_DIM)
    query_here = queries.reshape(shaped)
    grad_here = out_grad.reshape(shaped)
    count = lax.axis_size("ctx")
    shifts = offset_list(count)
    scaling = HEAD_DIM ** (-0.5)
    blocks_seen = len(shifts)
    fetched = [shifted((key_rows, value_rows), "ctx", -offset) for offset in shifts[1:]]
    key_stack = jnp.stack([key_rows] + [pair[0] for pair in fetched]).reshape(
        (blocks_seen,) + shaped
    )
    value_stack = jnp.stack([value_rows] + [pair[1] for pair in fetched]).reshape(
        (blocks_seen,) + shaped
    )

    def pass_one(carry, key_block):
        peak, total = carry
        scores = block_scores(query_here, key_block, scaling)
        new_peak = jnp.maximum(peak, scores.max(-1))
        total = total * jnp.exp(peak - new_peak) + jnp.exp(scores - new_peak[..., None]).sum(-1)
        return ((new_peak, total), None)

    start_peak = jnp.full((heads_here, rows), -jnp.inf, jnp.float32)
    start_total = jnp.zeros((heads_here, rows), jnp.float32)
    (peak, total), unused = lax.scan(pass_one, (start_peak, start_total), key_stack)
    row_lse = peak + jnp.log(total)

    def pass_two(summed, blocks):
        key_block, value_block = blocks
        weights = jnp.exp(block_scores(query_here, key_block, scaling) - row_lse[..., None]).astype(
            jnp.bfloat16
        )
        summed = summed + jnp.einsum(
            "hqk,khd->qhd", weights, value_block, preferred_element_type=jnp.float32
        )
        return (summed, None)

    summed, unused = lax.scan(pass_two, jnp.zeros(shaped, jnp.float32), (key_stack, value_stack))
    attended = summed.astype(jnp.bfloat16)
    delta = jnp.einsum("qhd,qhd->hq", grad_here.astype(jnp.float32), attended.astype(jnp.float32))

    def query_side(key_block, value_block):
        probs = jnp.exp(block_scores(query_here, key_block, scaling) - row_lse[..., None])
        weights = probs.astype(jnp.bfloat16)
        dprob = jnp.einsum(
            "qhd,khd->hqk", grad_here, value_block, preferred_element_type=jnp.float32
        )
        dscore = (probs * (dprob - delta[..., None])).astype(jnp.bfloat16)
        return (weights, dscore)

    def pass_three(query_sum, blocks):
        key_block, value_block = blocks
        weights, dscore = query_side(key_block, value_block)
        query_sum = query_sum + jnp.einsum(
            "hqk,khd->qhd", dscore, key_block, preferred_element_type=jnp.float32
        )
        key_term = (
            jnp.einsum("hqk,qhd->khd", dscore, query_here, preferred_element_type=jnp.float32)
            * scaling
        ).astype(jnp.bfloat16)
        value_term = jnp.einsum(
            "hqk,qhd->khd", weights, grad_here, preferred_element_type=jnp.float32
        ).astype(jnp.bfloat16)
        return (query_sum, (key_term, value_term))

    query_sum, terms = lax.scan(
        pass_three, jnp.zeros(shaped, jnp.float32), (key_stack, value_stack)
    )
    key_terms, value_terms = terms
    key_sum = lax.optimization_barrier(key_terms[0]).astype(jnp.float32)
    value_sum = lax.optimization_barrier(value_terms[0]).astype(jnp.float32)
    for index in range(1, blocks_seen):
        moved = shifted((key_terms[index], value_terms[index]), "ctx", shifts[index])
        key_sum = key_sum + moved[0].astype(jnp.float32)
        value_sum = value_sum + moved[1].astype(jnp.float32)
    flat = (rows, width_all)
    return (
        attended.reshape(flat),
        (query_sum * scaling).astype(jnp.bfloat16).reshape(flat),
        key_sum.astype(jnp.bfloat16).reshape(flat),
        value_sum.astype(jnp.bfloat16).reshape(flat),
    )


def dot(a, b, dims):
    return lax.dot_general(a, b, (dims, ((), ())), preferred_element_type=jnp.float32)


def exchange_kernel(
    n,
    shifts,
    q_in,
    k_in,
    v_in,
    g_in,
    o_out,
    dq_out,
    dk_out,
    dv_out,
    qb,
    kb,
    vb,
    gb,
    qt,
    gt,
    wb,
    sb,
    ob,
    dqb,
    dkb,
    dvb,
    in_send,
    in_recv,
    out_send,
    out_recv,
    ends_sem,
):
    me = lax.axis_index("ctx")
    scaling = HEAD_DIM ** (-0.5)

    def partner(d):
        total, bit = 0, 1
        while bit < n:
            total = total + bit * ((me // bit + d // bit) % 2)
            bit *= 2
        return total

    quarter = n // 4
    same = [s for s in range(1, n) if s // quarter in (0, 3)]
    opposite = 3 * quarter
    beside = range(quarter, 2 * quarter)
    zone = me // quarter
    middle = jnp.logical_or(zone == 1, zone == 2)

    def tell(sem, s):
        pl.semaphore_signal(
            sem, inc=1, device_id={"ctx": partner(s)}, device_id_type=pl.DeviceIdType.MESH
        )

    barrier = pltpu.get_barrier_semaphore()

    tell(barrier, opposite)

    @pl.when(jnp.logical_not(middle))
    def _():
        for s in same:
            if s != opposite:
                tell(barrier, s)

    def columns(index):
        return pl.ds(pl.multiple_of(index * HEAD_DIM, HEAD_DIM), HEAD_DIM)

    inward = ((k_in, kb), (q_in, qb), (v_in, vb), (g_in, gb))
    outward = ((ob, o_out), (dvb, dv_out), (dqb, dq_out), (dkb, dk_out))

    def in_copy(t, s):
        source, place = inward[t]
        peer = partner(s)
        return pltpu.make_async_remote_copy(
            src_ref=source.at[:, columns(peer)],
            dst_ref=place.at[me],
            send_sem=in_send.at[t],
            recv_sem=in_recv.at[t],
            device_id={"ctx": peer},
            device_id_type=pl.DeviceIdType.MESH,
        )

    def in_own(t):
        source, place = inward[t]
        return pltpu.make_async_copy(source.at[:, columns(me)], place.at[me], in_recv.at[t])

    def out_copy(t, s):
        source, place = outward[t]
        peer = partner(s)
        return pltpu.make_async_remote_copy(
            src_ref=source.at[peer],
            dst_ref=place.at[:, columns(me)],
            send_sem=out_send.at[t],
            recv_sem=out_recv.at[t],
            device_id={"ctx": peer},
            device_id_type=pl.DeviceIdType.MESH,
        )

    def out_own(t):
        source, place = outward[t]
        return pltpu.make_async_copy(source.at[me], place.at[:, columns(me)], out_recv.at[t])

    def start(peers):
        for t in range(4):
            for s in peers:
                in_copy(t, s).start()

    @pl.when(middle)
    def _():
        pl.semaphore_wait(barrier, 1)
        for s in beside:
            tell(barrier, s)
        start([opposite])
        pl.semaphore_wait(ends_sem, 1)
        start([s for s in reversed(same) if s != opposite])
        start([s for s in range(n - 1, 0, -1) if s not in same])

    @pl.when(jnp.logical_not(middle))
    def _():
        pl.semaphore_wait(barrier, len(same) + quarter)
        tell(ends_sem, quarter)
        start(range(n - 1, 0, -1))

    for t in range(4):
        in_own(t).start()

    def arrive(t):
        whole = inward[t][1]
        pltpu.make_async_copy(whole, whole, in_recv.at[t]).wait()

    def each_block(body):
        lax.fori_loop(0, n, lambda step, c: (body(step), c)[1], 0)

    low = [*range(2 * quarter), 3 * quarter, *range(2 * quarter, 3 * quarter)]
    low += range(3 * quarter + 1, n)
    high = [*range(quarter), *range(2 * quarter, n), *range(quarter, 2 * quarter)]

    def pick(order, step):
        block = order[-1]
        for k in range(n - 1):
            block = jnp.where(step == k, order[k], block)
        return block

    def flips(step):
        return partner(jnp.where(zone < 2, pick(low, step), pick(high, step)))

    def send(t, step):
        s = flips(step)

        @pl.when(s > 0)
        def _():
            out_copy(t, s).start()

        @pl.when(s == 0)
        def _():
            out_own(t).start()

    def near(index, sign=1):
        return [lax.rem(index + sign * d + n, n) for d in shifts]

    def rows_of(buf, index):
        return jnp.concatenate([buf[j] for j in near(index)], axis=0)

    arrive(0)
    arrive(1)

    def scores(i):
        q = qb[i]
        s = dot(q, rows_of(kb, i), ((1,), (1,)))
        peak = jnp.max(s, axis=-1, keepdims=True)
        e = jnp.exp2((s - peak) * (scaling * math.log2(math.e)))
        w = (e * (1.0 / jnp.sum(e, axis=-1, keepdims=True))).astype(jnp.bfloat16)
        for m in range(len(shifts)):
            wb[i, m] = w[:, m * 128 : (m + 1) * 128]
        qt[i] = q.T

    each_block(scores)
    arrive(2)

    def block_weights(ref, i):
        return jnp.concatenate([ref[i, m] for m in range(len(shifts))], axis=1)

    def attend(step):
        i = partner(flips(step))
        o = dot(block_weights(wb, i), rows_of(vb, i), ((1,), (0,)))
        ob[i] = o.astype(jnp.bfloat16)
        send(0, step)

    each_block(attend)
    arrive(3)

    def transpose_grad(i):
        gt[i] = gb[i].T

    each_block(transpose_grad)

    def value_side(step):
        j = partner(flips(step))
        from_blocks = near(j, -1)
        left = jnp.concatenate([gt[i] for i in from_blocks], axis=1)
        right = jnp.concatenate([wb[i, m] for m, i in enumerate(from_blocks)], axis=0)
        dvb[j] = dot(left, right, ((1,), (0,))).T.astype(jnp.bfloat16)
        send(1, step)

    each_block(value_side)

    def query_side(step):
        i = partner(flips(step))
        g = gb[i]
        delta = jnp.sum(g.astype(jnp.float32) * ob[i].astype(jnp.float32), axis=-1, keepdims=True)
        dprob = dot(g, rows_of(vb, i), ((1,), (1,)))
        ds = (block_weights(wb, i).astype(jnp.float32) * (dprob - delta)).astype(jnp.bfloat16)
        for m in range(len(shifts)):
            sb[i, m] = ds[:, m * 128 : (m + 1) * 128]
        dqb[i] = (dot(ds, rows_of(kb, i), ((1,), (0,))) * scaling).astype(jnp.bfloat16)

    each_block(query_side)

    def key_side(step):
        j = partner(flips(step))
        from_blocks = near(j, -1)
        left = jnp.concatenate([qt[i] for i in from_blocks], axis=1)
        right = jnp.concatenate([sb[i, m] for m, i in enumerate(from_blocks)], axis=0)
        dkb[j] = (dot(left, right, ((1,), (0,))) * scaling).T.astype(jnp.bfloat16)
        send(2, step)
        send(3, step)

    each_block(key_side)

    for t in range(4):
        sent = inward[t][1].at[pl.ds(0, n - 1)]
        pltpu.make_async_copy(sent, sent, in_send.at[t]).wait()
    for t in range(4):
        sent = outward[t][0].at[pl.ds(0, n - 1)]
        pltpu.make_async_copy(sent, sent, out_send.at[t]).wait()
        whole = outward[t][1]
        pltpu.make_async_copy(whole, whole, out_recv.at[t]).wait()


def exchanged(queries, key_rows, value_rows, out_grad):
    rows = queries.shape[0]
    n = lax.axis_size("ctx")
    shifts = offset_list(n)
    seen = len(shifts)
    block = (n, rows, HEAD_DIM)
    bf16 = jnp.bfloat16
    return pl.pallas_call(
        functools.partial(exchange_kernel, n, shifts),
        out_shape=tuple(jax.ShapeDtypeStruct(queries.shape, bf16) for _ in range(4)),
        in_specs=[pl.BlockSpec(memory_space=pltpu.HBM)] * 4,
        out_specs=tuple(pl.BlockSpec(memory_space=pl.ANY) for _ in range(4)),
        scratch_shapes=[pltpu.VMEM(block, bf16)] * 4
        + [pltpu.VMEM((n, HEAD_DIM, rows), bf16)] * 2
        + [pltpu.VMEM((n, seen, rows, rows), bf16)] * 2
        + [pltpu.VMEM(block, bf16)] * 4
        + [pltpu.SemaphoreType.DMA((4,))] * 4
        + [pltpu.SemaphoreType.REGULAR],
        compiler_params=pltpu.CompilerParams(
            collective_id=0, has_side_effects=True, vmem_limit_bytes=40 * 2**20
        ),
    )(*[pltpu.with_memory_space_constraint(x, pltpu.HBM) for x in (queries, key_rows, value_rows, out_grad)])


def store_kernel(*refs):
    sems = refs[8]
    copies = [pltpu.make_async_copy(refs[t], refs[4 + t], sems.at[t]) for t in range(4)]
    for c in copies:
        c.start()
    for c in copies:
        c.wait()


def stored(arrays):
    return pl.pallas_call(
        store_kernel,
        out_shape=tuple(jax.ShapeDtypeStruct(a.shape, a.dtype) for a in arrays),
        in_specs=[pl.BlockSpec(memory_space=pl.ANY)] * 4,
        out_specs=tuple(pl.BlockSpec(memory_space=pl.ANY) for _ in range(4)),
        scratch_shapes=[pltpu.SemaphoreType.DMA((4,))],
    )(*[pltpu.with_memory_space_constraint(a, pltpu.VMEM) for a in arrays])


def per_device(queries, key_rows, value_rows, out_grad):
    rows, width = queries.shape
    count = lax.axis_size("ctx")
    if rows == HEAD_DIM and count * HEAD_DIM == width and count >= 4 and count & (count - 1) == 0:
        return tuple(stored(exchanged(queries, key_rows, value_rows, out_grad)))
    return permuted(queries, key_rows, value_rows, out_grad)


def solution(mesh):
    return jax.shard_map(
        per_device,
        mesh=mesh,
        in_specs=(
            P(("groups", "ctx"), "head"),
            P(("groups", "ctx"), "head"),
            P(("groups", "ctx"), "head"),
            P(("groups", "ctx"), "head"),
        ),
        out_specs=(
            P(("groups", "ctx"), "head"),
            P(("groups", "ctx"), "head"),
            P(("groups", "ctx"), "head"),
            P(("groups", "ctx"), "head"),
        ),
        check_vma=False,
    )
```

```python
import functools
import math

import jax
import jax.numpy as jnp
from jax import lax
from jax.experimental import pallas as pl
from jax.experimental.pallas import tpu as pltpu
from jax.sharding import PartitionSpec as P

HEAD_DIM = 128


def shifted(block, axis, distance):
    devices = range(lax.axis_size(axis))
    route = [((i - distance) % len(devices), i) for i in devices]
    return lax.ppermute(block, axis, route)


def offset_list(count):
    result = [0]
    width = 1
    while width < count // 2:
        result = result + [width, -width]
        width = width * 2
    result.append(count // 2)
    return result


def block_scores(query_part, key_part, scaling):
    return (
        jnp.einsum("qhd,khd->hqk", query_part, key_part, preferred_element_type=jnp.float32)
        * scaling
    )


def permuted(queries, key_rows, value_rows, out_grad):
    rows = queries.shape[0]
    width_all = queries.shape[1]
    heads_here = width_all // HEAD_DIM
    shaped = (rows, heads_here, HEAD_DIM)
    query_here = queries.reshape(shaped)
    grad_here = out_grad.reshape(shaped)
    count = lax.axis_size("ctx")
    shifts = offset_list(count)
    scaling = HEAD_DIM ** (-0.5)
    blocks_seen = len(shifts)
    fetched = [shifted((key_rows, value_rows), "ctx", -offset) for offset in shifts[1:]]
    key_stack = jnp.stack([key_rows] + [pair[0] for pair in fetched]).reshape(
        (blocks_seen,) + shaped
    )
    value_stack = jnp.stack([value_rows] + [pair[1] for pair in fetched]).reshape(
        (blocks_seen,) + shaped
    )

    def pass_one(carry, key_block):
        peak, total = carry
        scores = block_scores(query_here, key_block, scaling)
        new_peak = jnp.maximum(peak, scores.max(-1))
        total = total * jnp.exp(peak - new_peak) + jnp.exp(scores - new_peak[..., None]).sum(-1)
        return ((new_peak, total), None)

    start_peak = jnp.full((heads_here, rows), -jnp.inf, jnp.float32)
    start_total = jnp.zeros((heads_here, rows), jnp.float32)
    (peak, total), unused = lax.scan(pass_one, (start_peak, start_total), key_stack)
    row_lse = peak + jnp.log(total)

    def pass_two(summed, blocks):
        key_block, value_block = blocks
        weights = jnp.exp(block_scores(query_here, key_block, scaling) - row_lse[..., None]).astype(
            jnp.bfloat16
        )
        summed = summed + jnp.einsum(
            "hqk,khd->qhd", weights, value_block, preferred_element_type=jnp.float32
        )
        return (summed, None)

    summed, unused = lax.scan(pass_two, jnp.zeros(shaped, jnp.float32), (key_stack, value_stack))
    attended = summed.astype(jnp.bfloat16)
    delta = jnp.einsum("qhd,qhd->hq", grad_here.astype(jnp.float32), attended.astype(jnp.float32))

    def query_side(key_block, value_block):
        probs = jnp.exp(block_scores(query_here, key_block, scaling) - row_lse[..., None])
        weights = probs.astype(jnp.bfloat16)
        dprob = jnp.einsum(
            "qhd,khd->hqk", grad_here, value_block, preferred_element_type=jnp.float32
        )
        dscore = (probs * (dprob - delta[..., None])).astype(jnp.bfloat16)
        return (weights, dscore)

    def pass_three(query_sum, blocks):
        key_block, value_block = blocks
        weights, dscore = query_side(key_block, value_block)
        query_sum = query_sum + jnp.einsum(
            "hqk,khd->qhd", dscore, key_block, preferred_element_type=jnp.float32
        )
        key_term = (
            jnp.einsum("hqk,qhd->khd", dscore, query_here, preferred_element_type=jnp.float32)
            * scaling
        ).astype(jnp.bfloat16)
        value_term = jnp.einsum(
            "hqk,qhd->khd", weights, grad_here, preferred_element_type=jnp.float32
        ).astype(jnp.bfloat16)
        return (query_sum, (key_term, value_term))

    query_sum, terms = lax.scan(
        pass_three, jnp.zeros(shaped, jnp.float32), (key_stack, value_stack)
    )
    key_terms, value_terms = terms
    key_sum = lax.optimization_barrier(key_terms[0]).astype(jnp.float32)
    value_sum = lax.optimization_barrier(value_terms[0]).astype(jnp.float32)
    for index in range(1, blocks_seen):
        moved = shifted((key_terms[index], value_terms[index]), "ctx", shifts[index])
        key_sum = key_sum + moved[0].astype(jnp.float32)
        value_sum = value_sum + moved[1].astype(jnp.float32)
    flat = (rows, width_all)
    return (
        attended.reshape(flat),
        (query_sum * scaling).astype(jnp.bfloat16).reshape(flat),
        key_sum.astype(jnp.bfloat16).reshape(flat),
        value_sum.astype(jnp.bfloat16).reshape(flat),
    )


def dot(a, b, dims):
    return lax.dot_general(a, b, (dims, ((), ())), preferred_element_type=jnp.float32)


def exchange_kernel(
    n,
    shifts,
    q_in,
    k_in,
    v_in,
    g_in,
    o_out,
    dq_out,
    dk_out,
    dv_out,
    qb,
    kb,
    vb,
    gb,
    qt,
    gt,
    wb,
    sb,
    ob,
    dqb,
    dkb,
    dvb,
    in_send,
    in_recv,
    out_send,
    out_recv,
    ends_sem,
):
    me = lax.axis_index("ctx")
    scaling = HEAD_DIM ** (-0.5)

    def partner(d):
        total, bit = 0, 1
        while bit < n:
            total = total + bit * ((me // bit + d // bit) % 2)
            bit *= 2
        return total

    quarter = n // 4
    same = [s for s in range(1, n) if s // quarter in (0, 3)]
    opposite = 3 * quarter
    beside = range(quarter, 2 * quarter)
    zone = me // quarter
    middle = jnp.logical_or(zone == 1, zone == 2)

    def tell(sem, s):
        pl.semaphore_signal(
            sem, inc=1, device_id={"ctx": partner(s)}, device_id_type=pl.DeviceIdType.MESH
        )

    barrier = pltpu.get_barrier_semaphore()

    tell(barrier, opposite)

    @pl.when(jnp.logical_not(middle))
    def _():
        for s in same:
            if s != opposite:
                tell(barrier, s)

    def columns(index):
        return pl.ds(pl.multiple_of(index * HEAD_DIM, HEAD_DIM), HEAD_DIM)

    inward = ((k_in, kb), (q_in, qb), (v_in, vb), (g_in, gb))
    outward = ((ob, o_out), (dvb, dv_out), (dqb, dq_out), (dkb, dk_out))

    def in_copy(t, s):
        source, place = inward[t]
        peer = partner(s)
        return pltpu.make_async_remote_copy(
            src_ref=source.at[:, columns(peer)],
            dst_ref=place.at[me],
            send_sem=in_send.at[t],
            recv_sem=in_recv.at[t],
            device_id={"ctx": peer},
            device_id_type=pl.DeviceIdType.MESH,
        )

    def in_own(t):
        source, place = inward[t]
        return pltpu.make_async_copy(source.at[:, columns(me)], place.at[me], in_recv.at[t])

    def out_copy(t, s):
        source, place = outward[t]
        peer = partner(s)
        return pltpu.make_async_remote_copy(
            src_ref=source.at[peer],
            dst_ref=place.at[:, columns(me)],
            send_sem=out_send.at[t],
            recv_sem=out_recv.at[t],
            device_id={"ctx": peer},
            device_id_type=pl.DeviceIdType.MESH,
        )

    def out_own(t):
        source, place = outward[t]
        return pltpu.make_async_copy(source.at[me], place.at[:, columns(me)], out_recv.at[t])

    def start(peers, tensors=range(4)):
        for t in tensors:
            for s in peers:
                in_copy(t, s).start()

    @pl.when(middle)
    def _():
        pl.semaphore_wait(barrier, 1)
        for s in beside:
            tell(barrier, s)
        start([opposite])
        pl.semaphore_wait(ends_sem, 1)
        start([s for s in reversed(same) if s != opposite])
        start([s for s in range(n - 1, 0, -1) if s not in same])

    @pl.when(jnp.logical_not(middle))
    def _():
        pl.semaphore_wait(barrier, len(same) + quarter)
        tell(ends_sem, quarter)
        start(range(n - 1, 0, -1), (0, 1))
        far_middle = range(3 * quarter - 1, 2 * quarter - 1, -1)
        far_end = range(n - 1, 3 * quarter - 1, -1)
        start([*far_middle, *far_end, *range(2 * quarter - 1, 0, -1)], (2, 3))

    for t in range(4):
        in_own(t).start()

    def arrive(t):
        whole = inward[t][1]
        pltpu.make_async_copy(whole, whole, in_recv.at[t]).wait()

    def each_block(body):
        lax.fori_loop(0, n, lambda step, c: (body(step), c)[1], 0)

    low = [*range(2 * quarter), 3 * quarter, *range(2 * quarter, 3 * quarter)]
    low += range(3 * quarter + 1, n)
    high = [*range(quarter), *range(2 * quarter, n), *range(quarter, 2 * quarter)]

    def pick(order, step):
        block = order[-1]
        for k in range(n - 1):
            block = jnp.where(step == k, order[k], block)
        return block

    def flips(step):
        return partner(jnp.where(zone < 2, pick(low, step), pick(high, step)))

    def send(t, step):
        s = flips(step)

        @pl.when(s > 0)
        def _():
            out_copy(t, s).start()

        @pl.when(s == 0)
        def _():
            out_own(t).start()

    def near(index, sign=1):
        return [lax.rem(index + sign * d + n, n) for d in shifts]

    def rows_of(buf, index):
        return jnp.concatenate([buf[j] for j in near(index)], axis=0)

    arrive(0)
    arrive(1)

    def scores(i):
        q = qb[i]
        s = dot(q, rows_of(kb, i), ((1,), (1,)))
        peak = jnp.max(s, axis=-1, keepdims=True)
        e = jnp.exp2((s - peak) * (scaling * math.log2(math.e)))
        w = (e * (1.0 / jnp.sum(e, axis=-1, keepdims=True))).astype(jnp.bfloat16)
        for m in range(len(shifts)):
            wb[i, m] = w[:, m * 128 : (m + 1) * 128]
        qt[i] = q.T

    each_block(scores)
    arrive(2)

    def block_weights(ref, i):
        return jnp.concatenate([ref[i, m] for m in range(len(shifts))], axis=1)

    def attend(step):
        i = partner(flips(step))
        o = dot(block_weights(wb, i), rows_of(vb, i), ((1,), (0,)))
        ob[i] = o.astype(jnp.bfloat16)
        send(0, step)

    each_block(attend)
    arrive(3)

    def transpose_grad(i):
        gt[i] = gb[i].T

    each_block(transpose_grad)

    def value_side(step):
        j = partner(flips(step))
        from_blocks = near(j, -1)
        left = jnp.concatenate([gt[i] for i in from_blocks], axis=1)
        right = jnp.concatenate([wb[i, m] for m, i in enumerate(from_blocks)], axis=0)
        dvb[j] = dot(left, right, ((1,), (0,))).T.astype(jnp.bfloat16)
        send(1, step)

    each_block(value_side)

    def query_side(step):
        i = partner(flips(step))
        g = gb[i]
        delta = jnp.sum(g.astype(jnp.float32) * ob[i].astype(jnp.float32), axis=-1, keepdims=True)
        dprob = dot(g, rows_of(vb, i), ((1,), (1,)))
        ds = (block_weights(wb, i).astype(jnp.float32) * (dprob - delta)).astype(jnp.bfloat16)
        for m in range(len(shifts)):
            sb[i, m] = ds[:, m * 128 : (m + 1) * 128]
        dqb[i] = (dot(ds, rows_of(kb, i), ((1,), (0,))) * scaling).astype(jnp.bfloat16)

    each_block(query_side)

    def key_side(step):
        j = partner(flips(step))
        from_blocks = near(j, -1)
        left = jnp.concatenate([qt[i] for i in from_blocks], axis=1)
        right = jnp.concatenate([sb[i, m] for m, i in enumerate(from_blocks)], axis=0)
        dkb[j] = (dot(left, right, ((1,), (0,))) * scaling).T.astype(jnp.bfloat16)
        send(2, step)
        send(3, step)

    each_block(key_side)

    for t in range(4):
        sent = inward[t][1].at[pl.ds(0, n - 1)]
        pltpu.make_async_copy(sent, sent, in_send.at[t]).wait()
    for t in range(4):
        sent = outward[t][0].at[pl.ds(0, n - 1)]
        pltpu.make_async_copy(sent, sent, out_send.at[t]).wait()
        whole = outward[t][1]
        pltpu.make_async_copy(whole, whole, out_recv.at[t]).wait()


def exchanged(queries, key_rows, value_rows, out_grad):
    rows = queries.shape[0]
    n = lax.axis_size("ctx")
    shifts = offset_list(n)
    seen = len(shifts)
    block = (n, rows, HEAD_DIM)
    bf16 = jnp.bfloat16
    return pl.pallas_call(
        functools.partial(exchange_kernel, n, shifts),
        out_shape=tuple(jax.ShapeDtypeStruct(queries.shape, bf16) for _ in range(4)),
        in_specs=[pl.BlockSpec(memory_space=pltpu.HBM)] * 4,
        out_specs=tuple(pl.BlockSpec(memory_space=pl.ANY) for _ in range(4)),
        scratch_shapes=[pltpu.VMEM(block, bf16)] * 4
        + [pltpu.VMEM((n, HEAD_DIM, rows), bf16)] * 2
        + [pltpu.VMEM((n, seen, rows, rows), bf16)] * 2
        + [pltpu.VMEM(block, bf16)] * 4
        + [pltpu.SemaphoreType.DMA((4,))] * 4
        + [pltpu.SemaphoreType.REGULAR],
        compiler_params=pltpu.CompilerParams(
            collective_id=0, has_side_effects=True, vmem_limit_bytes=40 * 2**20
        ),
    )(*[pltpu.with_memory_space_constraint(x, pltpu.HBM) for x in (queries, key_rows, value_rows, out_grad)])


def store_kernel(*refs):
    sems = refs[8]
    copies = [pltpu.make_async_copy(refs[t], refs[4 + t], sems.at[t]) for t in range(4)]
    for c in copies:
        c.start()
    for c in copies:
        c.wait()


def stored(arrays):
    return pl.pallas_call(
        store_kernel,
        out_shape=tuple(jax.ShapeDtypeStruct(a.shape, a.dtype) for a in arrays),
        in_specs=[pl.BlockSpec(memory_space=pl.ANY)] * 4,
        out_specs=tuple(pl.BlockSpec(memory_space=pl.ANY) for _ in range(4)),
        scratch_shapes=[pltpu.SemaphoreType.DMA((4,))],
    )(*[pltpu.with_memory_space_constraint(a, pltpu.VMEM) for a in arrays])


def per_device(queries, key_rows, value_rows, out_grad):
    rows, width = queries.shape
    count = lax.axis_size("ctx")
    if rows == HEAD_DIM and count * HEAD_DIM == width and count >= 4 and count & (count - 1) == 0:
        return tuple(stored(exchanged(queries, key_rows, value_rows, out_grad)))
    return permuted(queries, key_rows, value_rows, out_grad)


def solution(mesh):
    return jax.shard_map(
        per_device,
        mesh=mesh,
        in_specs=(
            P(("groups", "ctx"), "head"),
            P(("groups", "ctx"), "head"),
            P(("groups", "ctx"), "head"),
            P(("groups", "ctx"), "head"),
        ),
        out_specs=(
            P(("groups", "ctx"), "head"),
            P(("groups", "ctx"), "head"),
            P(("groups", "ctx"), "head"),
            P(("groups", "ctx"), "head"),
        ),
        check_vma=False,
    )
```

```python
import functools
import math

import jax
import jax.numpy as jnp
from jax import lax
from jax.experimental import pallas as pl
from jax.experimental.pallas import tpu as pltpu
from jax.sharding import PartitionSpec as P

HEAD_DIM = 128


def shifted(block, axis, distance):
    devices = range(lax.axis_size(axis))
    route = [((i - distance) % len(devices), i) for i in devices]
    return lax.ppermute(block, axis, route)


def offset_list(count):
    result = [0]
    width = 1
    while width < count // 2:
        result = result + [width, -width]
        width = width * 2
    result.append(count // 2)
    return result


def block_scores(query_part, key_part, scaling):
    return (
        jnp.einsum("qhd,khd->hqk", query_part, key_part, preferred_element_type=jnp.float32)
        * scaling
    )


def permuted(queries, key_rows, value_rows, out_grad):
    rows = queries.shape[0]
    width_all = queries.shape[1]
    heads_here = width_all // HEAD_DIM
    shaped = (rows, heads_here, HEAD_DIM)
    query_here = queries.reshape(shaped)
    grad_here = out_grad.reshape(shaped)
    count = lax.axis_size("ctx")
    shifts = offset_list(count)
    scaling = HEAD_DIM ** (-0.5)
    blocks_seen = len(shifts)
    fetched = [shifted((key_rows, value_rows), "ctx", -offset) for offset in shifts[1:]]
    key_stack = jnp.stack([key_rows] + [pair[0] for pair in fetched]).reshape(
        (blocks_seen,) + shaped
    )
    value_stack = jnp.stack([value_rows] + [pair[1] for pair in fetched]).reshape(
        (blocks_seen,) + shaped
    )

    def pass_one(carry, key_block):
        peak, total = carry
        scores = block_scores(query_here, key_block, scaling)
        new_peak = jnp.maximum(peak, scores.max(-1))
        total = total * jnp.exp(peak - new_peak) + jnp.exp(scores - new_peak[..., None]).sum(-1)
        return ((new_peak, total), None)

    start_peak = jnp.full((heads_here, rows), -jnp.inf, jnp.float32)
    start_total = jnp.zeros((heads_here, rows), jnp.float32)
    (peak, total), unused = lax.scan(pass_one, (start_peak, start_total), key_stack)
    row_lse = peak + jnp.log(total)

    def pass_two(summed, blocks):
        key_block, value_block = blocks
        weights = jnp.exp(block_scores(query_here, key_block, scaling) - row_lse[..., None]).astype(
            jnp.bfloat16
        )
        summed = summed + jnp.einsum(
            "hqk,khd->qhd", weights, value_block, preferred_element_type=jnp.float32
        )
        return (summed, None)

    summed, unused = lax.scan(pass_two, jnp.zeros(shaped, jnp.float32), (key_stack, value_stack))
    attended = summed.astype(jnp.bfloat16)
    delta = jnp.einsum("qhd,qhd->hq", grad_here.astype(jnp.float32), attended.astype(jnp.float32))

    def query_side(key_block, value_block):
        probs = jnp.exp(block_scores(query_here, key_block, scaling) - row_lse[..., None])
        weights = probs.astype(jnp.bfloat16)
        dprob = jnp.einsum(
            "qhd,khd->hqk", grad_here, value_block, preferred_element_type=jnp.float32
        )
        dscore = (probs * (dprob - delta[..., None])).astype(jnp.bfloat16)
        return (weights, dscore)

    def pass_three(query_sum, blocks):
        key_block, value_block = blocks
        weights, dscore = query_side(key_block, value_block)
        query_sum = query_sum + jnp.einsum(
            "hqk,khd->qhd", dscore, key_block, preferred_element_type=jnp.float32
        )
        key_term = (
            jnp.einsum("hqk,qhd->khd", dscore, query_here, preferred_element_type=jnp.float32)
            * scaling
        ).astype(jnp.bfloat16)
        value_term = jnp.einsum(
            "hqk,qhd->khd", weights, grad_here, preferred_element_type=jnp.float32
        ).astype(jnp.bfloat16)
        return (query_sum, (key_term, value_term))

    query_sum, terms = lax.scan(
        pass_three, jnp.zeros(shaped, jnp.float32), (key_stack, value_stack)
    )
    key_terms, value_terms = terms
    key_sum = lax.optimization_barrier(key_terms[0]).astype(jnp.float32)
    value_sum = lax.optimization_barrier(value_terms[0]).astype(jnp.float32)
    for index in range(1, blocks_seen):
        moved = shifted((key_terms[index], value_terms[index]), "ctx", shifts[index])
        key_sum = key_sum + moved[0].astype(jnp.float32)
        value_sum = value_sum + moved[1].astype(jnp.float32)
    flat = (rows, width_all)
    return (
        attended.reshape(flat),
        (query_sum * scaling).astype(jnp.bfloat16).reshape(flat),
        key_sum.astype(jnp.bfloat16).reshape(flat),
        value_sum.astype(jnp.bfloat16).reshape(flat),
    )


def dot(a, b, dims):
    return lax.dot_general(a, b, (dims, ((), ())), preferred_element_type=jnp.float32)


def exchange_kernel(
    n,
    shifts,
    q_in,
    k_in,
    v_in,
    g_in,
    o_out,
    dq_out,
    dk_out,
    dv_out,
    qb,
    kb,
    vb,
    gb,
    qt,
    gt,
    wb,
    sb,
    ob,
    dqb,
    dkb,
    dvb,
    in_send,
    in_recv,
    out_send,
    out_recv,
    ends_sem,
):
    me = lax.axis_index("ctx")
    scaling = HEAD_DIM ** (-0.5)

    def partner(d):
        total, bit = 0, 1
        while bit < n:
            total = total + bit * ((me // bit + d // bit) % 2)
            bit *= 2
        return total

    quarter = n // 4
    same = [s for s in range(1, n) if s // quarter in (0, 3)]
    opposite = 3 * quarter
    beside = range(quarter, 2 * quarter)
    zone = me // quarter
    middle = jnp.logical_or(zone == 1, zone == 2)

    def tell(sem, s):
        pl.semaphore_signal(
            sem, inc=1, device_id={"ctx": partner(s)}, device_id_type=pl.DeviceIdType.MESH
        )

    barrier = pltpu.get_barrier_semaphore()

    tell(barrier, opposite)

    @pl.when(jnp.logical_not(middle))
    def _():
        for s in same:
            if s != opposite:
                tell(barrier, s)

    def columns(index):
        return pl.ds(pl.multiple_of(index * HEAD_DIM, HEAD_DIM), HEAD_DIM)

    inward = ((k_in, kb), (q_in, qb), (v_in, vb), (g_in, gb))
    outward = ((ob, o_out), (dvb, dv_out), (dqb, dq_out), (dkb, dk_out))

    def in_copy(t, s):
        source, place = inward[t]
        peer = partner(s)
        return pltpu.make_async_remote_copy(
            src_ref=source.at[:, columns(peer)],
            dst_ref=place.at[me],
            send_sem=in_send.at[t],
            recv_sem=in_recv.at[t],
            device_id={"ctx": peer},
            device_id_type=pl.DeviceIdType.MESH,
        )

    def in_own(t):
        source, place = inward[t]
        return pltpu.make_async_copy(source.at[:, columns(me)], place.at[me], in_recv.at[t])

    def out_copy(t, s):
        source, place = outward[t]
        peer = partner(s)
        return pltpu.make_async_remote_copy(
            src_ref=source.at[peer],
            dst_ref=place.at[:, columns(me)],
            send_sem=out_send.at[t],
            recv_sem=out_recv.at[t],
            device_id={"ctx": peer},
            device_id_type=pl.DeviceIdType.MESH,
        )

    def out_own(t):
        source, place = outward[t]
        return pltpu.make_async_copy(source.at[me], place.at[:, columns(me)], out_recv.at[t])

    def start(peers):
        for t in range(4):
            for s in peers:
                in_copy(t, s).start()

    @pl.when(middle)
    def _():
        pl.semaphore_wait(barrier, 1)
        for s in beside:
            tell(barrier, s)
        start([opposite])
        pl.semaphore_wait(ends_sem, 1)
        start([s for s in reversed(same) if s != opposite])
        start([s for s in range(n - 1, 0, -1) if s not in same])

    @pl.when(jnp.logical_not(middle))
    def _():
        pl.semaphore_wait(barrier, len(same) + quarter)
        tell(ends_sem, quarter)
        start(range(n - 1, 0, -1))


    def arrive(t):
        in_own(t).start()
        whole = inward[t][1]
        pltpu.make_async_copy(whole, whole, in_recv.at[t]).wait()

    def each_block(body):
        lax.fori_loop(0, n, lambda step, c: (body(step), c)[1], 0)

    low = [*range(2 * quarter), 3 * quarter, *range(2 * quarter, 3 * quarter)]
    low += range(3 * quarter + 1, n)
    high = [*range(quarter), *range(2 * quarter, n), *range(quarter, 2 * quarter)]

    def pick(order, step):
        block = order[-1]
        for k in range(n - 1):
            block = jnp.where(step == k, order[k], block)
        return block

    def flips(step):
        return partner(jnp.where(zone < 2, pick(low, step), pick(high, step)))

    def send(t, step):
        s = flips(step)

        @pl.when(s > 0)
        def _():
            out_copy(t, s).start()

        @pl.when(s == 0)
        def _():
            out_own(t).start()

    def near(index, sign=1):
        return [lax.rem(index + sign * d + n, n) for d in shifts]

    def rows_of(buf, index):
        return jnp.concatenate([buf[j] for j in near(index)], axis=0)

    arrive(0)
    arrive(1)

    def scores(i):
        q = qb[i]
        s = dot(q, rows_of(kb, i), ((1,), (1,)))
        peak = jnp.max(s, axis=-1, keepdims=True)
        e = jnp.exp2((s - peak) * (scaling * math.log2(math.e)))
        w = (e * (1.0 / jnp.sum(e, axis=-1, keepdims=True))).astype(jnp.bfloat16)
        for m in range(len(shifts)):
            wb[i, m] = w[:, m * 128 : (m + 1) * 128]
        qt[i] = q.T

    each_block(scores)
    arrive(2)

    def block_weights(ref, i):
        return jnp.concatenate([ref[i, m] for m in range(len(shifts))], axis=1)

    def attend(step):
        i = partner(flips(step))
        o = dot(block_weights(wb, i), rows_of(vb, i), ((1,), (0,)))
        ob[i] = o.astype(jnp.bfloat16)
        send(0, step)

    each_block(attend)
    arrive(3)

    def transpose_grad(i):
        gt[i] = gb[i].T

    each_block(transpose_grad)

    def value_side(step):
        j = partner(flips(step))
        from_blocks = near(j, -1)
        left = jnp.concatenate([gt[i] for i in from_blocks], axis=1)
        right = jnp.concatenate([wb[i, m] for m, i in enumerate(from_blocks)], axis=0)
        dvb[j] = dot(left, right, ((1,), (0,))).T.astype(jnp.bfloat16)
        send(1, step)

    each_block(value_side)

    def query_side(step):
        i = partner(flips(step))
        g = gb[i]
        delta = jnp.sum(g.astype(jnp.float32) * ob[i].astype(jnp.float32), axis=-1, keepdims=True)
        dprob = dot(g, rows_of(vb, i), ((1,), (1,)))
        ds = (block_weights(wb, i).astype(jnp.float32) * (dprob - delta)).astype(jnp.bfloat16)
        for m in range(len(shifts)):
            sb[i, m] = ds[:, m * 128 : (m + 1) * 128]
        dqb[i] = (dot(ds, rows_of(kb, i), ((1,), (0,))) * scaling).astype(jnp.bfloat16)

    each_block(query_side)

    def key_side(step):
        j = partner(flips(step))
        from_blocks = near(j, -1)
        left = jnp.concatenate([qt[i] for i in from_blocks], axis=1)
        right = jnp.concatenate([sb[i, m] for m, i in enumerate(from_blocks)], axis=0)
        dkb[j] = (dot(left, right, ((1,), (0,))) * scaling).T.astype(jnp.bfloat16)
        send(2, step)
        send(3, step)

    each_block(key_side)

    for t in range(4):
        sent = inward[t][1].at[pl.ds(0, n - 1)]
        pltpu.make_async_copy(sent, sent, in_send.at[t]).wait()
    for t in range(4):
        sent = outward[t][0].at[pl.ds(0, n - 1)]
        pltpu.make_async_copy(sent, sent, out_send.at[t]).wait()
        whole = outward[t][1]
        pltpu.make_async_copy(whole, whole, out_recv.at[t]).wait()


def exchanged(queries, key_rows, value_rows, out_grad):
    rows = queries.shape[0]
    n = lax.axis_size("ctx")
    shifts = offset_list(n)
    seen = len(shifts)
    block = (n, rows, HEAD_DIM)
    bf16 = jnp.bfloat16
    return pl.pallas_call(
        functools.partial(exchange_kernel, n, shifts),
        out_shape=tuple(jax.ShapeDtypeStruct(queries.shape, bf16) for _ in range(4)),
        in_specs=[pl.BlockSpec(memory_space=pltpu.HBM)] * 4,
        out_specs=tuple(pl.BlockSpec(memory_space=pl.ANY) for _ in range(4)),
        scratch_shapes=[pltpu.VMEM(block, bf16)] * 4
        + [pltpu.VMEM((n, HEAD_DIM, rows), bf16)] * 2
        + [pltpu.VMEM((n, seen, rows, rows), bf16)] * 2
        + [pltpu.VMEM(block, bf16)] * 4
        + [pltpu.SemaphoreType.DMA((4,))] * 4
        + [pltpu.SemaphoreType.REGULAR],
        compiler_params=pltpu.CompilerParams(
            collective_id=0, has_side_effects=True, vmem_limit_bytes=40 * 2**20
        ),
    )(*[pltpu.with_memory_space_constraint(x, pltpu.HBM) for x in (queries, key_rows, value_rows, out_grad)])


def store_kernel(*refs):
    sems = refs[8]
    copies = [pltpu.make_async_copy(refs[t], refs[4 + t], sems.at[t]) for t in range(4)]
    for c in copies:
        c.start()
    for c in copies:
        c.wait()


def stored(arrays):
    return pl.pallas_call(
        store_kernel,
        out_shape=tuple(jax.ShapeDtypeStruct(a.shape, a.dtype) for a in arrays),
        in_specs=[pl.BlockSpec(memory_space=pl.ANY)] * 4,
        out_specs=tuple(pl.BlockSpec(memory_space=pl.ANY) for _ in range(4)),
        scratch_shapes=[pltpu.SemaphoreType.DMA((4,))],
    )(*[pltpu.with_memory_space_constraint(a, pltpu.VMEM) for a in arrays])


def per_device(queries, key_rows, value_rows, out_grad):
    rows, width = queries.shape
    count = lax.axis_size("ctx")
    if rows == HEAD_DIM and count * HEAD_DIM == width and count >= 4 and count & (count - 1) == 0:
        return tuple(stored(exchanged(queries, key_rows, value_rows, out_grad)))
    return permuted(queries, key_rows, value_rows, out_grad)


def solution(mesh):
    return jax.shard_map(
        per_device,
        mesh=mesh,
        in_specs=(
            P(("groups", "ctx"), "head"),
            P(("groups", "ctx"), "head"),
            P(("groups", "ctx"), "head"),
            P(("groups", "ctx"), "head"),
        ),
        out_specs=(
            P(("groups", "ctx"), "head"),
            P(("groups", "ctx"), "head"),
            P(("groups", "ctx"), "head"),
            P(("groups", "ctx"), "head"),
        ),
        check_vma=False,
    )
```
